32 devices in a mesh: gx: 4 (over z), gy: 8 (over y, x, core).
Axes of the slice: x: 2, y: 2, z: 4, core: 2. Of those that a mesh axis runs over, the one named last changes fastest.
Arguments:
- populations: float32 [19, 64, 32, 128], P(None, 'gx', 'gy'), as said below
- vert_base: int32 [3, 16384], P(None, ('gx', 'gy')), may hold values from 0 to 127, as said below
- vert_frac: float32 [3, 16384], P(None, ('gx', 'gy')), may hold values from 0 to 0.999
- edges: int32 [2, 49152], P(None, ('gx', 'gy')), may hold values from 0 to 511, as said below
- stiffness: float32 [49152], P(('gx', 'gy')), may hold values from 0.05 to 0.5
- rest: float32 [3, 49152], P(None, ('gx', 'gy')), may hold values from -3 to 3
Outputs:
- fresh: float32 [19, 64, 32, 128], P(None, 'gx', 'gy')
- vertex_velocity: float32 [3, 16384], P(None, ('gx', 'gy'))
The draws below stay inside these ranges and needn't reach their ends.
Inputs may be any that keep to these rules, and one draw needn't show every extreme that they name: `vert_base`: the first coordinate lies below 64, the second below 32, the third below 128. The vertices are in blocks of 512, block k belonging to the k-th device in the order gx then gy; a vertex's first coordinate lies in that device's 16 cells along x, its second in its 4 cells along y. Each run of 128 vertices of a block lies in a box of 4 x 4 x 4 cells, periodic in z. `edges`: edge e belongs to block e // 1536; its two entries are distinct indices within that block's 512 vertices, both in the same run of 128 vertices. `populations`: every entry lies between 0.6 and 1.4 times the lattice weight of its direction.
All inputs are finite; a program needn't handle non-finite values.
Results may differ from the reference program's by a relative error of at most 0.000078.
Values sent between devices are 32-bit elements; how exact they have to be, the bound alone decides.
A program may use at most 64 MiB of HBM per device.

```python
import math
import jax
import jax.numpy as jnp
import numpy as np
from jax import lax

CX = 16
CY = 4
NZ = 128
VERT_DEV = 512
TILE = 128
NX = 64
NY = 32
VERTS = 16384
EDGE_DEV = 1536
EDGES = 49152


table_weights = np.array([1.0 / 3.0] + [1.0 / 18.0] * 6 + [1.0 / 36.0] * 12, np.float32)


def draw_populations(key, part):
    shape = (19, NX, NY, NZ)
    noise = jax.random.uniform(key, shape, jnp.float32, -0.38, 0.38)
    weights = jnp.asarray(table_weights, jnp.float32)[:, None, None, None]
    return weights * (1.0 + noise)


def draw_vert_base(key, part):
    tile_count = VERTS // TILE
    column_count = NY // CY
    vertex = jnp.arange(VERTS, dtype=jnp.int32)
    block = vertex // VERT_DEV
    tile = vertex // TILE
    tile_x = jax.random.randint(jax.random.fold_in(key, 11), (tile_count,), 0, CX - 3)
    tile_y = jax.random.randint(jax.random.fold_in(key, 12), (tile_count,), 0, CY - 3)
    tile_z = jax.random.randint(jax.random.fold_in(key, 13), (tile_count,), 0, NZ)
    spread = jax.random.randint(jax.random.fold_in(key, 14), (3, VERTS), 0, 4)
    first = block // column_count * CX + tile_x[tile] + spread[0]
    second = block % column_count * CY + tile_y[tile] + spread[1]
    third = (tile_z[tile] + spread[2]) % NZ
    return jnp.stack([first, second, third]).astype(jnp.int32)


def draw_edges(key, part):
    local = jnp.arange(EDGES, dtype=jnp.int32) % EDGE_DEV
    group = local // (3 * TILE)
    start = jax.random.randint(jax.random.fold_in(key, 21), (EDGES,), 0, TILE)
    stride = jax.random.randint(jax.random.fold_in(key, 22), (EDGES,), 1, TILE)
    first = group * TILE + start
    second = group * TILE + (start + stride) % TILE
    return jnp.stack([first, second]).astype(jnp.int32)


def levels(rng, extent, pieces, smallest, largest):
    gain = 1.0
    for dim, shards_of in pieces:
        steps = jax.random.uniform(jax.random.fold_in(jax.random.fold_in(rng, 6), dim), (shards_of,), jnp.float32, smallest / len(pieces), largest / len(pieces))
        gain = gain * jnp.repeat(jnp.exp(steps), extent[dim] // shards_of).reshape((-1,) + (1,) * (len(extent) - 1 - dim))
    return gain


def centred(stream_key, shape, scale, most, pieces=(), kind=jnp.bfloat16):
    factor_of = levels(stream_key, shape, pieces, -0.22, 0.18) if pieces else 1.0
    drawn = jax.random.normal(stream_key, shape, jnp.float32) * scale * factor_of
    return jnp.minimum(jnp.maximum(drawn, -most), most).astype(kind)


def setup_inputs(seed: int = 0) -> dict:
    streams_of = jax.random.split(jax.random.key(seed), 7)
    return {
        "populations": draw_populations(jax.random.fold_in(streams_of[6], 71), 0),
        "vert_base": draw_vert_base(jax.random.fold_in(streams_of[6], 71), 0),
        "vert_frac": jnp.clip(0.999 * jax.random.uniform(streams_of[2], (3, VERTS), jnp.float32) ** levels(streams_of[2], (3, VERTS), ((1, 32),), -0.2, 0.2), 0.0, 0.999),
        "edges": draw_edges(jax.random.fold_in(streams_of[6], 71), 0),
        "stiffness": jnp.clip(jnp.exp(math.log(0.5) - 2.3025851 * jax.random.uniform(streams_of[4], (EDGES,), jnp.float32) ** levels(streams_of[4], (EDGES,), ((0, 32),), -0.2, 0.2)), 0.05, 0.5),
        "rest": centred(streams_of[5], (3, EDGES), 0.5, 3.0, ((1, 32),), jnp.float32),
    }


lattice_speeds = [(0, 0, 0), (1, 0, 0), (-1, 0, 0), (0, 1, 0), (0, -1, 0), (0, 0, 1), (0, 0, -1), (1, 1, 0), (-1, -1, 0), (1, -1, 0), (-1, 1, 0), (1, 0, 1), (-1, 0, -1), (1, 0, -1), (-1, 0, 1), (0, 1, 1), (0, -1, -1), (0, 1, -1), (0, -1, 1)]
lattice_weights = [1.0 / 3.0] + [1.0 / 18.0] * 6 + [1.0 / 36.0] * 12
relax_time = 0.9

def outer_weight(r):
    return (5.0 - 2.0 * r - jnp.sqrt(-7.0 + 12.0 * r - 4.0 * r * r)) / 8.0

def inner_weight(r):
    return (3.0 - 2.0 * r + jnp.sqrt(1.0 + 4.0 * r - 4.0 * r * r)) / 8.0

def kernel_weights(frac):
    return jnp.stack([outer_weight(1.0 + frac), inner_weight(frac), inner_weight(1.0 - frac), outer_weight(2.0 - frac)])

def collide(popul, force):
    speeds = jnp.asarray(lattice_speeds, jnp.float32)
    weights = jnp.asarray(lattice_weights, jnp.float32)[:, None, None, None]
    high = lax.Precision.HIGHEST
    density = lax.optimization_barrier(jnp.sum(popul, axis=0))
    moment = jnp.tensordot(speeds.T, popul, axes=1, precision=high)
    velocity = (moment + 0.5 * force) / density
    along = jnp.tensordot(speeds, velocity, axes=1, precision=high)
    square = lax.optimization_barrier(jnp.sum(velocity * velocity, axis=0))
    balance = weights * density * (1.0 + 3.0 * along + 4.5 * along * along - 1.5 * square)
    push = jnp.tensordot(speeds, force, axes=1, precision=high)
    work = lax.optimization_barrier(jnp.sum(velocity * force, axis=0))
    source = (1.0 - 0.5 / relax_time) * weights * (3.0 * (push - work) + 9.0 * along * push)
    post = popul - (popul - balance) / relax_time + source
    return (post, velocity)

def reference(populations, vert_base, vert_frac, edges, stiffness, rest):
    position = vert_base.astype(jnp.float32) + vert_frac
    offset = jnp.arange(EDGES, dtype=jnp.int32) // EDGE_DEV * VERT_DEV
    first = edges[0] + offset
    second = edges[1] + offset
    stretch = stiffness[None, :] * (position[:, second] - position[:, first] - rest)
    membrane = jnp.zeros((3, VERTS), jnp.float32).at[:, first].add(stretch).at[:, second].add(-stretch)
    kernel = kernel_weights(vert_frac)
    grid = jnp.zeros((3, NX, NY, NZ), jnp.float32)
    cells = []
    for kx in range(4):
        for ky in range(4):
            for kz in range(4):
                index_x = (vert_base[0] - 1 + kx) % NX
                index_y = (vert_base[1] - 1 + ky) % NY
                index_z = (vert_base[2] - 1 + kz) % NZ
                weight = kernel[kx, 0] * kernel[ky, 1] * kernel[kz, 2]
                cells.append((index_x, index_y, index_z, weight))
                grid = grid.at[:, index_x, index_y, index_z].add(membrane * weight[None, :])
    post, velocity = collide(populations, grid)
    rows = []
    for q in range(19):
        shift = lattice_speeds[q]
        rows.append(jnp.roll(post[q], shift, axis=(0, 1, 2)))
    fresh = jnp.stack(rows)
    sampled = jnp.zeros((3, VERTS), jnp.float32)
    for index_x, index_y, index_z, weight in cells:
        sampled = sampled + velocity[:, index_x, index_y, index_z] * weight[None, :]
    return (fresh, sampled)
```

```python
import jax
import jax.numpy as jnp
from jax import lax
from jax.experimental import pallas as pl
from jax.experimental.pallas import tpu as pltpu
from jax.sharding import PartitionSpec as P

lattice_speeds = [
    (0, 0, 0),
    (1, 0, 0),
    (-1, 0, 0),
    (0, 1, 0),
    (0, -1, 0),
    (0, 0, 1),
    (0, 0, -1),
    (1, 1, 0),
    (-1, -1, 0),
    (1, -1, 0),
    (-1, 1, 0),
    (1, 0, 1),
    (-1, 0, -1),
    (1, 0, -1),
    (-1, 0, 1),
    (0, 1, 1),
    (0, -1, -1),
    (0, 1, -1),
    (0, -1, 1),
]
lattice_weights = [1.0 / 3.0] + [1.0 / 18.0] * 6 + [1.0 / 36.0] * 12
relax_time = 0.9
run = 128
sides = [(1, 0), (-1, 0), (0, 1), (0, -1), (1, 1), (1, -1), (-1, 1), (-1, -1)]
f32, bf16 = jnp.float32, jnp.bfloat16


def outer_weight(r):
    return (5.0 - 2.0 * r - jnp.sqrt(-7.0 + 12.0 * r - 4.0 * r * r)) / 8.0


def inner_weight(r):
    return (3.0 - 2.0 * r + jnp.sqrt(1.0 + 4.0 * r - 4.0 * r * r)) / 8.0


def up8(n):
    return (n + 7) // 8 * 8


class Plan:
    def __init__(self, wx, wy):
        self.wx, self.wy = wx, wy
        self.own = wx * wy
        self.xh = self.own
        self.yh = self.xh + 4 * wy
        self.co = self.yh + 3 * wx
        self.rows = self.co + 16
        hx, hy = [-1, wx, wx + 1], [-1, wy, wy + 1]
        self.row = {}
        for x in range(wx):
            for y in range(wy):
                self.row[x, y] = x * wy + y
        for k in range(3):
            for y in range(wy):
                self.row[hx[k], y] = self.xh + k * wy + y
            for x in range(wx):
                self.row[x, hy[k]] = self.yh + k * wx + x
            for m in range(3):
                self.row[hx[m], hy[k]] = self.co + 3 * k + m
        self.pads = [(self.xh + 3 * wy, wy), (self.co + 9, 7)]

        def span(d, w):
            full = list(range(w)) + [-1, w, w + 1]
            return {0: full, 1: [w - 1, w, w + 1], -1: [-1, 0, 1]}[d]

        def edge(d, w):
            return {0: list(range(w)), 1: [w - 1], -1: [0, 1]}[d]

        def near(d, w):
            return {0: list(range(w)), 1: [w - 1], -1: [0]}[d]

        def cells(d, pick):
            xs, ys = pick(d[0], wx), pick(d[1], wy)
            if d[1]:
                return [(x, y) for y in ys for x in xs]
            return [(x, y) for x in xs for y in ys]

        self.force = [cells(d, span) for d in sides]
        self.edge = [cells(d, edge) for d in sides]
        self.near = [cells(d, near) for d in sides]
        self.dirs = [
            [
                q
                for q, c in enumerate(lattice_speeds)
                if (not d[0] or c[0] == d[0]) and (not d[1] or c[1] == d[1])
            ]
            for d in sides
        ]
        self.force_rows = [up8(3 * len(c)) for c in self.force]
        self.macro_rows = [
            up8(4 * len(e) + len(q) * len(n)) for e, q, n in zip(self.edge, self.dirs, self.near)
        ]

    def there(self, cell, d):
        return self.row[cell[0] - d[0] * self.wx, cell[1] - d[1] * self.wy]


def runs(src, dst):
    out, i = [], 0
    while i < len(src):
        n, a, b = 1, 1, 1
        if i + 1 < len(src) and src[i + 1] > src[i] and dst[i + 1] > dst[i]:
            a, b = src[i + 1] - src[i], dst[i + 1] - dst[i]
            n = 2
            while i + n < len(src) and src[i + n] - src[i + n - 1] == a and dst[i + n] - dst[i + n - 1] == b:
                n += 1
        out.append((src[i], a, dst[i], b, n))
        i += n
    return out


def ds(start, n, stride):
    return pl.ds(start, n, stride=stride) if stride > 1 else pl.ds(start, n)


def move(src_ref, src, dst_ref, dst, add=False):
    for s, a, d, b, n in runs(src, dst):
        value = src_ref[ds(s, n, a), :]
        if add:
            value = value + dst_ref[ds(d, n, b), :]
        dst_ref[ds(d, n, b), :] = value


def split(value):
    high = value.astype(bf16)
    return high, (value - high.astype(f32)).astype(bf16)


def pick4(delta, weights):
    out = jnp.zeros(delta.shape, f32)
    for k in range(4):
        out = jnp.where(delta == k, weights[k], out)
    return out


def step_kernel(plan, nx, ny, pops, base, frac, edges, stiff, rest, fresh, sampled, *scratch):
    wx, wy, rows, own = plan.wx, plan.wy, plan.rows, plan.own
    ms, mr, fs, fr = scratch[0:8], scratch[8:16], scratch[16:24], scratch[24:32]
    ext, grid, halo, post, plane, along, pos, pull, mem, vel, sems = scratch[32:]
    count, depth = base.shape[1], pops.shape[1]
    edge_count = edges.shape[1]
    tiles = count // run
    ix, iy = lax.axis_index("gx"), lax.axis_index("gy")
    peers = [(lax.rem(ix + dx + nx, nx), lax.rem(iy + dy + ny, ny)) for dx, dy in sides]
    barrier = pltpu.get_barrier_semaphore()
    for peer in peers:
        pl.semaphore_signal(barrier, inc=1, device_id=peer, device_id_type=pl.DeviceIdType.MESH)

    def copies(src, dst, kind):
        return [
            pltpu.make_async_remote_copy(
                src_ref=src[n],
                dst_ref=dst[n],
                send_sem=sems.at[kind, n],
                recv_sem=sems.at[kind + 1, n],
                device_id=peers[n],
                device_id_type=pl.DeviceIdType.MESH,
            )
            for n in range(8)
        ]

    macro_copies = copies(ms, mr, 0)
    force_copies = copies(fs, fr, 2)

    for r in range(0, own, 16):
        totals = [None] * 4
        for q, c in enumerate(lattice_speeds):
            value = pops[pl.ds(q * own + r, 16), :]
            for k, sign in enumerate((1,) + c):
                if sign:
                    term = value if sign > 0 else -value
                    totals[k] = term if totals[k] is None else totals[k] + term
        for k in range(4):
            ext[pl.ds(k * rows + r, 16), :] = totals[k]
    for start, n in plan.pads:
        for k in range(4):
            ext[pl.ds(k * rows + start, n), :] = jnp.full((n, depth), 0.0 if k else 1.0, f32)
    for n in range(8):
        cells, close = plan.edge[n], plan.near[n]
        for k in range(4):
            move(ext, [k * rows + plan.row[c] for c in cells], ms[n], [k * len(cells) + i for i in range(len(cells))])
        for s, q in enumerate(plan.dirs[n]):
            first = 4 * len(cells) + s * len(close)
            move(pops, [q * own + plan.row[c] for c in close], ms[n], [first + i for i in range(len(close))])

    pos[...] = jnp.zeros(pos.shape, f32)
    part = 8 * tiles
    moved = frac[...]
    high = moved.astype(bf16).astype(f32)
    low = moved - high
    whole = base[...].astype(f32)
    for t in range(tiles):
        cols = slice(t * run, (t + 1) * run)
        pos[pl.ds(8 * t, 3), :] = whole[:, cols]
        pos[pl.ds(part + 8 * t, 3), :] = high[:, cols]
        pos[pl.ds(2 * part + 8 * t, 3), :] = low[:, cols]
    ends = edges[...]
    spot = lax.broadcasted_iota(jnp.int32, (run, edge_count), 0)
    tail = jnp.bitwise_and(ends[0:1], run - 1)
    head = jnp.bitwise_and(ends[1:2], run - 1)
    hot = (jnp.where(spot == head, 1.0, 0.0) - jnp.where(spot == tail, 1.0, 0.0)).astype(bf16)
    group = lax.shift_right_logical(ends[0:1], run.bit_length() - 1)
    reach = jnp.dot(pos[...].astype(bf16), hot, preferred_element_type=f32)
    reach = reach[0:part] + reach[part : 2 * part] + reach[2 * part : 3 * part]
    pull[...] = jnp.zeros(pull.shape, f32)
    pull[pl.ds(0, 3), :] = rest[...]
    diff = jnp.zeros((8, edge_count), f32)
    for t in range(tiles):
        diff = jnp.where(group == t, reach[8 * t : 8 * t + 8], diff)
    stretch = stiff[...] * (diff - pull[...])
    terms = jnp.concatenate([jnp.where(group == t, stretch, 0.0) for t in range(tiles)], axis=0)
    big, small = split(terms)
    both = jnp.concatenate([big, small], axis=0)
    summed = lax.dot_general(both, hot, (((1,), (1,)), ((), ())), preferred_element_type=f32)
    summed = summed[0:part] + summed[part : 2 * part]
    for t in range(tiles):
        mem[:, t * run : (t + 1) * run] = -summed[8 * t : 8 * t + 8]

    pl.semaphore_wait(barrier, 8)
    for copy in macro_copies:
        copy.start()

    weights = [
        outer_weight(1.0 + moved),
        inner_weight(moved),
        inner_weight(1.0 - moved),
        outer_weight(2.0 - moved),
    ]
    bx = base[0:1, :] - ix * wx - 1
    by = base[1:2, :] - iy * wy - 1
    bz = base[2:3, :] - 1
    gap = lax.broadcasted_iota(jnp.int32, (depth, count), 0) - bz
    gap = jnp.where(gap < 0, gap + depth, gap)
    gap = jnp.where(gap >= depth, gap - depth, gap)
    along_z = pick4(gap, [w[2:3] for w in weights])
    z_high, z_low = split(along_z)
    along[pl.ds(0, depth), :] = z_high
    along[pl.ds(depth, depth), :] = z_low
    far = -100
    for r in range(0, rows, 16):
        i = lax.broadcasted_iota(jnp.int32, (16, 1), 0)
        if r < plan.xh:
            i = i + r
            x = i // wy
            y = i - x * wy
        elif r < plan.yh:
            i = i + (r - plan.xh)
            k = i // wy
            x = jnp.where(k == 0, -1, jnp.where(k == 3, far, wx - 1 + k))
            y = i - k * wy
        elif r < plan.co:
            k = (r - plan.yh) // wx
            x = i + (r - plan.yh - k * wx)
            y = jnp.full((16, 1), (-1, wy, wy + 1)[k], jnp.int32)
        else:
            k = jnp.where(i >= 6, 2, jnp.where(i >= 3, 1, 0))
            m = i - 3 * k
            x = jnp.where(m == 0, -1, jnp.where(m >= 3, far, wx - 1 + m))
            y = jnp.where(k == 0, -1, wy - 1 + k)
        px = pick4(x - bx, [w[0:1] for w in weights])
        py = pick4(y - by, [w[1:2] for w in weights])
        plane[pl.ds(r, 16), :] = px * py
    flat = plane[...]
    loads = [split(flat * mem[c : c + 1, :]) for c in range(3)]
    stack = jnp.concatenate([h for h, _ in loads] + [l for _, l in loads], axis=0)
    spread = lax.dot_general(stack, along[...], (((1,), (1,)), ((), ())), preferred_element_type=f32)
    spread = spread[0 : 3 * rows] + spread[3 * rows : 6 * rows]
    grid[...] = spread[:, 0:depth] + spread[:, depth : 2 * depth]
    for n in range(8):
        cells = plan.force[n]
        for k in range(3):
            move(grid, [k * rows + plan.row[c] for c in cells], fs[n], [k * len(cells) + i for i in range(len(cells))])
    for copy in force_copies:
        copy.start()

    for n in range(8):
        macro_copies[n].wait_recv()
        cells, close, d = plan.edge[n], plan.near[n], sides[n]
        for k in range(4):
            move(mr[n], [k * len(cells) + i for i in range(len(cells))], ext, [k * rows + plan.there(c, d) for c in cells])
        for s, q in enumerate(plan.dirs[n]):
            first = 4 * len(cells) + s * len(close)
            move(mr[n], [first + i for i in range(len(close))], halo, [q * rows + plan.there(c, d) for c in close])
    for n in range(8):
        force_copies[n].wait_recv()
        cells, d = plan.force[n], sides[n]
        for k in range(3):
            move(fr[n], [k * len(cells) + i for i in range(len(cells))], grid, [k * rows + plan.there(c, d) for c in cells], add=True)

    keep = 1.0 - 1.0 / relax_time
    half = 1.0 - 0.5 / relax_time

    def along_speed(c, vector):
        total = None
        for k in range(3):
            if c[k]:
                term = vector[k] if c[k] > 0 else -vector[k]
                total = term if total is None else total + term
        return total

    for r in range(0, rows, 16):
        density = ext[pl.ds(r, 16), :]
        force = [grid[pl.ds(k * rows + r, 16), :] for k in range(3)]
        inverse = 1.0 / density
        speed = [(ext[pl.ds((k + 1) * rows + r, 16), :] + 0.5 * force[k]) * inverse for k in range(3)]
        for k in range(3):
            vel[pl.ds(k * rows + r, 16), :] = speed[k]
        if r < own:
            need = list(range(19))
        elif r < plan.yh:
            need = [q for q in range(19) if lattice_speeds[q][0]]
        elif r < plan.yh + wx:
            need = [q for q in range(19) if lattice_speeds[q][1] == 1]
        elif r < plan.yh + 2 * wx:
            need = [q for q in range(19) if lattice_speeds[q][1] == -1]
        elif r < plan.co:
            continue
        else:
            need = [q for q in range(19) if lattice_speeds[q][0] and lattice_speeds[q][1]]
        square = speed[0] * speed[0] + speed[1] * speed[1] + speed[2] * speed[2]
        work = speed[0] * force[0] + speed[1] * force[1] + speed[2] * force[2]
        scaled = density * (1.0 / relax_time)
        level = scaled * (1.0 - 1.5 * square) - (3.0 * half) * work
        for first in [0] + list(range(1, 19, 2)):
            pair = [0] if first == 0 else [first, first + 1]
            if not any(q in need for q in pair):
                continue
            weight = lattice_weights[first]
            if first == 0:
                even, odd = level * weight, None
            else:
                a = along_speed(lattice_speeds[first], speed)
                push = along_speed(lattice_speeds[first], force)
                turn = scaled * a + half * push
                even = weight * (level + a * (4.5 * scaled * a + 9.0 * half * push))
                odd = (3.0 * weight) * turn
            for q in pair:
                if q not in need:
                    continue
                c = lattice_speeds[q]
                if r < own:
                    value = pops[pl.ds(q * own + r, 16), :]
                else:
                    value = halo[pl.ds(q * rows + r, 16), :]
                value = keep * value + even
                if odd is not None:
                    value = value + odd if q == first else value - odd
                if c[2]:
                    value = pltpu.roll(value, c[2] % depth, 1)
                if c[0] == 0 and c[1] == 0:
                    fresh[pl.ds(q * own + r, 16), :] = value
                else:
                    post[pl.ds(q * rows + r, 16), :] = value
    for q, c in enumerate(lattice_speeds):
        if c[0] == 0 and c[1] == 0:
            continue
        if c[1]:
            cells = [(x, y) for y in range(wy) for x in range(wx)]
        else:
            cells = [(x, y) for x in range(wx) for y in range(wy)]
        move(
            post,
            [q * rows + plan.row[x - c[0], y - c[1]] for x, y in cells],
            fresh,
            [q * own + x * wy + y for x, y in cells],
        )

    v_high, v_low = split(vel[...])
    value = jnp.dot(v_high, along[pl.ds(0, depth), :], preferred_element_type=f32)
    value = value + jnp.dot(v_low, along[pl.ds(0, depth), :], preferred_element_type=f32)
    value = value + jnp.dot(v_high, along[pl.ds(depth, depth), :], preferred_element_type=f32)
    flat = plane[...]
    for k in range(3):
        sampled[k : k + 1, :] = jnp.sum(value[k * rows : (k + 1) * rows] * flat, axis=0, keepdims=True)

    for copy in macro_copies + force_copies:
        copy.wait_send()


def solution(mesh):
    nx, ny = mesh.shape["gx"], mesh.shape["gy"]

    def per_device(populations, vert_base, vert_frac, edges, stiffness, rest):
        _, wx, wy, depth = populations.shape
        count, edge_count = vert_base.shape[1], edges.shape[1]
        plan = Plan(wx, wy)
        rows, tiles = plan.rows, count // run
        macro = [pltpu.VMEM((n, depth), f32) for n in plan.macro_rows]
        force = [pltpu.VMEM((n, depth), f32) for n in plan.force_rows]
        scratch = macro + macro + force + force
        scratch += [
            pltpu.VMEM((4 * rows, depth), f32),
            pltpu.VMEM((3 * rows, depth), f32),
            pltpu.VMEM((19 * rows, depth), f32),
            pltpu.VMEM((19 * rows, depth), f32),
            pltpu.VMEM((rows, count), f32),
            pltpu.VMEM((2 * depth, count), bf16),
            pltpu.VMEM((24 * tiles, run), f32),
            pltpu.VMEM((8, edge_count), f32),
            pltpu.VMEM((8, count), f32),
            pltpu.VMEM((3 * rows, depth), f32),
            pltpu.SemaphoreType.DMA((4, 8)),
        ]

        def body(*refs):
            step_kernel(plan, nx, ny, *refs)

        vmem = pl.BlockSpec(memory_space=pltpu.VMEM)
        fresh, sampled = pl.pallas_call(
            body,
            out_shape=(
                jax.ShapeDtypeStruct((19 * wx * wy, depth), f32),
                jax.ShapeDtypeStruct((3, count), f32),
            ),
            in_specs=[vmem] * 6,
            out_specs=(vmem, vmem),
            scratch_shapes=scratch,
            compiler_params=pltpu.CompilerParams(
                collective_id=0, has_side_effects=True, vmem_limit_bytes=48 * 1024 * 1024
            ),
            name="step",
        )(
            populations.reshape(19 * wx * wy, depth),
            vert_base,
            vert_frac,
            edges,
            stiffness.reshape(1, edge_count),
            rest,
        )
        return fresh.reshape(19, wx, wy, depth), sampled

    placed = (
        P(None, "gx", "gy", None),
        P(None, ("gx", "gy")),
        P(None, ("gx", "gy")),
        P(None, ("gx", "gy")),
        P(("gx", "gy")),
        P(None, ("gx", "gy")),
    )
    return jax.shard_map(
        per_device,
        mesh=mesh,
        in_specs=placed,
        out_specs=(P(None, "gx", "gy", None), P(None, ("gx", "gy"))),
        check_vma=False,
    )
```

```python
import jax
import jax.numpy as jnp
from jax import lax
from jax.experimental import pallas as pl
from jax.experimental.pallas import tpu as pltpu
from jax.sharding import PartitionSpec as P

lattice_speeds = [
    (0, 0, 0),
    (1, 0, 0),
    (-1, 0, 0),
    (0, 1, 0),
    (0, -1, 0),
    (0, 0, 1),
    (0, 0, -1),
    (1, 1, 0),
    (-1, -1, 0),
    (1, -1, 0),
    (-1, 1, 0),
    (1, 0, 1),
    (-1, 0, -1),
    (1, 0, -1),
    (-1, 0, 1),
    (0, 1, 1),
    (0, -1, -1),
    (0, 1, -1),
    (0, -1, 1),
]
lattice_weights = [1.0 / 3.0] + [1.0 / 18.0] * 6 + [1.0 / 36.0] * 12
relax_time = 0.9
run = 128
sides = [(1, 0), (-1, 0), (0, 1), (0, -1), (1, 1), (1, -1), (-1, 1), (-1, -1)]
f32, bf16 = jnp.float32, jnp.bfloat16


def outer_weight(r):
    return (5.0 - 2.0 * r - jnp.sqrt(-7.0 + 12.0 * r - 4.0 * r * r)) / 8.0


def inner_weight(r):
    return (3.0 - 2.0 * r + jnp.sqrt(1.0 + 4.0 * r - 4.0 * r * r)) / 8.0


def up8(n):
    return (n + 7) // 8 * 8


class Plan:
    def __init__(self, wx, wy):
        self.wx, self.wy = wx, wy
        self.own = wx * wy
        self.xh = self.own
        self.yh = self.xh + 4 * wy
        self.co = self.yh + 3 * wx
        self.rows = self.co + 16
        hx, hy = [-1, wx, wx + 1], [-1, wy, wy + 1]
        self.row = {}
        for x in range(wx):
            for y in range(wy):
                self.row[x, y] = x * wy + y
        for k in range(3):
            for y in range(wy):
                self.row[hx[k], y] = self.xh + k * wy + y
            for x in range(wx):
                self.row[x, hy[k]] = self.yh + k * wx + x
            for m in range(3):
                self.row[hx[m], hy[k]] = self.co + 3 * k + m
        self.pads = [(self.xh + 3 * wy, wy), (self.co + 9, 7)]

        def span(d, w):
            full = list(range(w)) + [-1, w, w + 1]
            return {0: full, 1: [w - 1, w, w + 1], -1: [-1, 0, 1]}[d]

        def edge(d, w):
            return {0: list(range(w)), 1: [w - 1], -1: [0, 1]}[d]

        def near(d, w):
            return {0: list(range(w)), 1: [w - 1], -1: [0]}[d]

        def cells(d, pick):
            xs, ys = pick(d[0], wx), pick(d[1], wy)
            if d[1]:
                return [(x, y) for y in ys for x in xs]
            return [(x, y) for x in xs for y in ys]

        self.force = [cells(d, span) for d in sides]
        self.edge = [cells(d, edge) for d in sides]
        self.near = [cells(d, near) for d in sides]
        self.dirs = [
            [
                q
                for q, c in enumerate(lattice_speeds)
                if (not d[0] or c[0] == d[0]) and (not d[1] or c[1] == d[1])
            ]
            for d in sides
        ]
        self.force_rows = [up8(3 * len(c)) for c in self.force]
        self.macro_rows = [
            up8(4 * len(e) + len(q) * len(n)) for e, q, n in zip(self.edge, self.dirs, self.near)
        ]

    def there(self, cell, d):
        return self.row[cell[0] - d[0] * self.wx, cell[1] - d[1] * self.wy]


def runs(src, dst):
    out, i = [], 0
    while i < len(src):
        n, a, b = 1, 1, 1
        if i + 1 < len(src) and src[i + 1] > src[i] and dst[i + 1] > dst[i]:
            a, b = src[i + 1] - src[i], dst[i + 1] - dst[i]
            n = 2
            while i + n < len(src) and src[i + n] - src[i + n - 1] == a and dst[i + n] - dst[i + n - 1] == b:
                n += 1
        out.append((src[i], a, dst[i], b, n))
        i += n
    return out


def ds(start, n, stride):
    return pl.ds(start, n, stride=stride) if stride > 1 else pl.ds(start, n)


def move(src_ref, src, dst_ref, dst, add=False):
    for s, a, d, b, n in runs(src, dst):
        value = src_ref[ds(s, n, a), :]
        if add:
            value = value + dst_ref[ds(d, n, b), :]
        dst_ref[ds(d, n, b), :] = value


def split(value):
    high = value.astype(bf16)
    return high, (value - high.astype(f32)).astype(bf16)


def pick4(delta, weights):
    out = jnp.zeros(delta.shape, f32)
    for k in range(4):
        out = jnp.where(delta == k, weights[k], out)
    return out


def exchange_kernel(plan, nx, ny, *refs):
    wx, wy, rows, own = plan.wx, plan.wy, plan.rows, plan.own
    sources, results, scratch = refs[0:6], refs[6:12], refs[12:]
    pops, ext, grid, halo, plane, along = results
    ms, mr, fs, fr = scratch[0:8], scratch[8:16], scratch[16:24], scratch[24:32]
    base, frac, edges, stiff, rest, pos, pull, mem, sems, load_sems = scratch[32:]
    targets = (pops, base, frac, edges, stiff, rest)
    loads_in = [pltpu.make_async_copy(sources[n], targets[n], load_sems.at[n]) for n in range(6)]
    for n in (3, 2, 1, 5, 4, 0):
        loads_in[n].start()
    count, depth = base.shape[1], pops.shape[1]
    edge_count = edges.shape[1]
    tiles = count // run
    ix, iy = lax.axis_index("gx"), lax.axis_index("gy")
    peers = [(lax.rem(ix + dx + nx, nx), lax.rem(iy + dy + ny, ny)) for dx, dy in sides]
    barrier = pltpu.get_barrier_semaphore()
    for peer in peers:
        pl.semaphore_signal(barrier, inc=1, device_id=peer, device_id_type=pl.DeviceIdType.MESH)

    def copies(src, dst, kind):
        return [
            pltpu.make_async_remote_copy(
                src_ref=src[n],
                dst_ref=dst[n],
                send_sem=sems.at[kind, n],
                recv_sem=sems.at[kind + 1, n],
                device_id=peers[n],
                device_id_type=pl.DeviceIdType.MESH,
            )
            for n in range(8)
        ]

    macro_copies = copies(ms, mr, 0)
    force_copies = copies(fs, fr, 2)

    pos[...] = jnp.zeros(pos.shape, f32)
    pull[...] = jnp.zeros(pull.shape, f32)
    for n in (3, 2, 1, 5, 4):
        loads_in[n].wait()
    part = 8 * tiles
    moved = frac[...]
    high = moved.astype(bf16).astype(f32)
    low = moved - high
    whole = base[...].astype(f32)
    for t in range(tiles):
        cols = slice(t * run, (t + 1) * run)
        pos[pl.ds(8 * t, 3), :] = whole[:, cols]
        pos[pl.ds(part + 8 * t, 3), :] = high[:, cols]
        pos[pl.ds(2 * part + 8 * t, 3), :] = low[:, cols]
    ends = edges[...]
    spot = lax.broadcasted_iota(jnp.int32, (run, edge_count), 0)
    tail = jnp.bitwise_and(ends[0:1], run - 1)
    head = jnp.bitwise_and(ends[1:2], run - 1)
    hot = (jnp.where(spot == head, 1.0, 0.0) - jnp.where(spot == tail, 1.0, 0.0)).astype(bf16)
    group = lax.shift_right_logical(ends[0:1], run.bit_length() - 1)
    reach = jnp.dot(pos[...].astype(bf16), hot, preferred_element_type=f32)
    reach = reach[0:part] + reach[part : 2 * part] + reach[2 * part : 3 * part]
    pull[pl.ds(0, 3), :] = rest[...]
    diff = jnp.zeros((8, edge_count), f32)
    for t in range(tiles):
        diff = jnp.where(group == t, reach[8 * t : 8 * t + 8], diff)
    stretch = stiff[...].reshape(1, edge_count) * (diff - pull[...])
    terms = jnp.concatenate([jnp.where(group == t, stretch, 0.0) for t in range(tiles)], axis=0)
    big, small = split(terms)
    both = jnp.concatenate([big, small], axis=0)
    summed = lax.dot_general(both, hot, (((1,), (1,)), ((), ())), preferred_element_type=f32)
    summed = summed[0:part] + summed[part : 2 * part]
    for t in range(tiles):
        mem[:, t * run : (t + 1) * run] = -summed[8 * t : 8 * t + 8]

    loads_in[0].wait()
    for r in range(0, own, 16):
        totals = [None] * 4
        for q, c in enumerate(lattice_speeds):
            value = pops[pl.ds(q * own + r, 16), :]
            for k, sign in enumerate((1,) + c):
                if sign:
                    term = value if sign > 0 else -value
                    totals[k] = term if totals[k] is None else totals[k] + term
        for k in range(4):
            ext[pl.ds(k * rows + r, 16), :] = totals[k]
    for start, n in plan.pads:
        for k in range(4):
            ext[pl.ds(k * rows + start, n), :] = jnp.full((n, depth), 0.0 if k else 1.0, f32)
    for n in range(8):
        cells, close = plan.edge[n], plan.near[n]
        for k in range(4):
            move(ext, [k * rows + plan.row[c] for c in cells], ms[n], [k * len(cells) + i for i in range(len(cells))])
        for s, q in enumerate(plan.dirs[n]):
            first = 4 * len(cells) + s * len(close)
            move(pops, [q * own + plan.row[c] for c in close], ms[n], [first + i for i in range(len(close))])

    pl.semaphore_wait(barrier, 8)
    for copy in macro_copies:
        copy.start()

    weights = [
        outer_weight(1.0 + moved),
        inner_weight(moved),
        inner_weight(1.0 - moved),
        outer_weight(2.0 - moved),
    ]
    bx = base[0:1, :] - ix * wx - 1
    by = base[1:2, :] - iy * wy - 1
    bz = base[2:3, :] - 1
    gap = lax.broadcasted_iota(jnp.int32, (depth, count), 0) - bz
    gap = jnp.where(gap < 0, gap + depth, gap)
    gap = jnp.where(gap >= depth, gap - depth, gap)
    along_z = pick4(gap, [w[2:3] for w in weights])
    z_high, z_low = split(along_z)
    along[pl.ds(0, depth), :] = z_high
    along[pl.ds(depth, depth), :] = z_low
    far = -100
    for r in range(0, rows, 16):
        i = lax.broadcasted_iota(jnp.int32, (16, 1), 0)
        if r < plan.xh:
            i = i + r
            x = i // wy
            y = i - x * wy
        elif r < plan.yh:
            i = i + (r - plan.xh)
            k = i // wy
            x = jnp.where(k == 0, -1, jnp.where(k == 3, far, wx - 1 + k))
            y = i - k * wy
        elif r < plan.co:
            k = (r - plan.yh) // wx
            x = i + (r - plan.yh - k * wx)
            y = jnp.full((16, 1), (-1, wy, wy + 1)[k], jnp.int32)
        else:
            k = jnp.where(i >= 6, 2, jnp.where(i >= 3, 1, 0))
            m = i - 3 * k
            x = jnp.where(m == 0, -1, jnp.where(m >= 3, far, wx - 1 + m))
            y = jnp.where(k == 0, -1, wy - 1 + k)
        px = pick4(x - bx, [w[0:1] for w in weights])
        py = pick4(y - by, [w[1:2] for w in weights])
        plane[pl.ds(r, 16), :] = px * py
    flat = plane[...]
    loads = [split(flat * mem[c : c + 1, :]) for c in range(3)]
    stack = jnp.concatenate([h for h, _ in loads] + [l for _, l in loads], axis=0)
    spread = lax.dot_general(stack, along[...], (((1,), (1,)), ((), ())), preferred_element_type=f32)
    spread = spread[0 : 3 * rows] + spread[3 * rows : 6 * rows]
    grid[...] = spread[:, 0:depth] + spread[:, depth : 2 * depth]
    for n in range(8):
        cells = plan.force[n]
        for k in range(3):
            move(grid, [k * rows + plan.row[c] for c in cells], fs[n], [k * len(cells) + i for i in range(len(cells))])
    for copy in force_copies:
        copy.start()

    for n in range(8):
        macro_copies[n].wait_recv()
        cells, close, d = plan.edge[n], plan.near[n], sides[n]
        for k in range(4):
            move(mr[n], [k * len(cells) + i for i in range(len(cells))], ext, [k * rows + plan.there(c, d) for c in cells])
        for s, q in enumerate(plan.dirs[n]):
            first = 4 * len(cells) + s * len(close)
            move(mr[n], [first + i for i in range(len(close))], halo, [q * rows + plan.there(c, d) for c in close])
    for n in range(8):
        force_copies[n].wait_recv()
        cells, d = plan.force[n], sides[n]
        for k in range(3):
            move(fr[n], [k * len(cells) + i for i in range(len(cells))], grid, [k * rows + plan.there(c, d) for c in cells], add=True)

    for copy in macro_copies + force_copies:
        copy.wait_send()


def collide_kernel(plan, pops, ext, grid, halo, plane, along, fresh_out, sampled_out, *scratch):
    wx, wy, rows, own = plan.wx, plan.wy, plan.rows, plan.own
    fresh, sampled, post, vel, sems = scratch
    depth = pops.shape[1]
    leave = [
        pltpu.make_async_copy(
            fresh.at[pl.ds(q * own, own), :], fresh_out.at[pl.ds(q * own, own), :], sems.at[q]
        )
        for q in range(19)
    ]
    leave.append(pltpu.make_async_copy(sampled, sampled_out, sems.at[19]))
    keep = 1.0 - 1.0 / relax_time
    half = 1.0 - 0.5 / relax_time

    def along_speed(c, vector):
        total = None
        for k in range(3):
            if c[k]:
                term = vector[k] if c[k] > 0 else -vector[k]
                total = term if total is None else total + term
        return total

    for r in range(0, rows, 16):
        density = ext[pl.ds(r, 16), :]
        force = [grid[pl.ds(k * rows + r, 16), :] for k in range(3)]
        inverse = 1.0 / density
        speed = [(ext[pl.ds((k + 1) * rows + r, 16), :] + 0.5 * force[k]) * inverse for k in range(3)]
        for k in range(3):
            vel[pl.ds(k * rows + r, 16), :] = speed[k]
        if r < own:
            need = list(range(19))
        elif r < plan.yh:
            need = [q for q in range(19) if lattice_speeds[q][0]]
        elif r < plan.yh + wx:
            need = [q for q in range(19) if lattice_speeds[q][1] == 1]
        elif r < plan.yh + 2 * wx:
            need = [q for q in range(19) if lattice_speeds[q][1] == -1]
        elif r < plan.co:
            continue
        else:
            need = [q for q in range(19) if lattice_speeds[q][0] and lattice_speeds[q][1]]
        square = speed[0] * speed[0] + speed[1] * speed[1] + speed[2] * speed[2]
        work = speed[0] * force[0] + speed[1] * force[1] + speed[2] * force[2]
        scaled = density * (1.0 / relax_time)
        level = scaled * (1.0 - 1.5 * square) - (3.0 * half) * work
        for first in [0] + list(range(1, 19, 2)):
            pair = [0] if first == 0 else [first, first + 1]
            if not any(q in need for q in pair):
                continue
            weight = lattice_weights[first]
            if first == 0:
                even, odd = level * weight, None
            else:
                a = along_speed(lattice_speeds[first], speed)
                push = along_speed(lattice_speeds[first], force)
                turn = scaled * a + half * push
                even = weight * (level + a * (4.5 * scaled * a + 9.0 * half * push))
                odd = (3.0 * weight) * turn
            for q in pair:
                if q not in need:
                    continue
                c = lattice_speeds[q]
                if r < own:
                    value = pops[pl.ds(q * own + r, 16), :]
                else:
                    value = halo[pl.ds(q * rows + r, 16), :]
                value = keep * value + even
                if odd is not None:
                    value = value + odd if q == first else value - odd
                if c[2]:
                    value = pltpu.roll(value, c[2] % depth, 1)
                if c[0] == 0 and c[1] == 0:
                    fresh[pl.ds(q * own + r, 16), :] = value
                else:
                    post[pl.ds(q * rows + r, 16), :] = value
    for q, c in enumerate(lattice_speeds):
        if c[0] == 0 and c[1] == 0:
            leave[q].start()
            continue
        if c[1]:
            cells = [(x, y) for y in range(wy) for x in range(wx)]
        else:
            cells = [(x, y) for x in range(wx) for y in range(wy)]
        move(
            post,
            [q * rows + plan.row[x - c[0], y - c[1]] for x, y in cells],
            fresh,
            [q * own + x * wy + y for x, y in cells],
        )
        leave[q].start()

    v_high, v_low = split(vel[...])
    value = jnp.dot(v_high, along[pl.ds(0, depth), :], preferred_element_type=f32)
    value = value + jnp.dot(v_low, along[pl.ds(0, depth), :], preferred_element_type=f32)
    value = value + jnp.dot(v_high, along[pl.ds(depth, depth), :], preferred_element_type=f32)
    flat = plane[...]
    for k in range(3):
        sampled[k : k + 1, :] = jnp.sum(value[k * rows : (k + 1) * rows] * flat, axis=0, keepdims=True)
    leave[19].start()
    for copy in leave:
        copy.wait()


def solution(mesh):
    nx, ny = mesh.shape["gx"], mesh.shape["gy"]

    def per_device(populations, vert_base, vert_frac, edges, stiffness, rest):
        _, wx, wy, depth = populations.shape
        count, edge_count = vert_base.shape[1], edges.shape[1]
        plan = Plan(wx, wy)
        rows, tiles = plan.rows, count // run
        macro = [pltpu.VMEM((n, depth), f32) for n in plan.macro_rows]
        force = [pltpu.VMEM((n, depth), f32) for n in plan.force_rows]
        scratch = macro + macro + force + force
        scratch += [
            pltpu.VMEM((3, count), jnp.int32),
            pltpu.VMEM((3, count), f32),
            pltpu.VMEM((2, edge_count), jnp.int32),
            pltpu.VMEM((edge_count,), f32),
            pltpu.VMEM((3, edge_count), f32),
            pltpu.VMEM((24 * tiles, run), f32),
            pltpu.VMEM((8, edge_count), f32),
            pltpu.VMEM((8, count), f32),
            pltpu.SemaphoreType.DMA((4, 8)),
            pltpu.SemaphoreType.DMA((6,)),
        ]
        vmem = pl.BlockSpec(memory_space=pltpu.VMEM)
        far = pl.BlockSpec(memory_space=pltpu.HBM)

        def exchange(*refs):
            exchange_kernel(plan, nx, ny, *refs)

        def collide(*refs):
            collide_kernel(plan, *refs)

        held = pl.pallas_call(
            exchange,
            out_shape=(
                jax.ShapeDtypeStruct((19 * wx * wy, depth), f32),
                jax.ShapeDtypeStruct((4 * rows, depth), f32),
                jax.ShapeDtypeStruct((3 * rows, depth), f32),
                jax.ShapeDtypeStruct((19 * rows, depth), f32),
                jax.ShapeDtypeStruct((rows, count), f32),
                jax.ShapeDtypeStruct((2 * depth, count), bf16),
            ),
            in_specs=[far] * 6,
            out_specs=(vmem,) * 6,
            scratch_shapes=scratch,
            compiler_params=pltpu.CompilerParams(
                collective_id=0, has_side_effects=True, vmem_limit_bytes=24 * 1024 * 1024
            ),
            name="exchange",
        )(
            *[
                pltpu.with_memory_space_constraint(value, pltpu.HBM)
                for value in (
                    populations.reshape(19 * wx * wy, depth),
                    vert_base,
                    vert_frac,
                    edges,
                    stiffness,
                    rest,
                )
            ]
        )
        fresh, sampled = pl.pallas_call(
            collide,
            out_shape=(
                jax.ShapeDtypeStruct((19 * wx * wy, depth), f32),
                jax.ShapeDtypeStruct((3, count), f32),
            ),
            in_specs=[vmem] * 6,
            out_specs=(far, far),
            scratch_shapes=[
                pltpu.VMEM((19 * wx * wy, depth), f32),
                pltpu.VMEM((3, count), f32),
                pltpu.VMEM((19 * rows, depth), f32),
                pltpu.VMEM((3 * rows, depth), f32),
                pltpu.SemaphoreType.DMA((20,)),
            ],
            compiler_params=pltpu.CompilerParams(vmem_limit_bytes=24 * 1024 * 1024),
            name="collide",
        )(*held)
        return fresh.reshape(19, wx, wy, depth), sampled

    placed = (
        P(None, "gx", "gy", None),
        P(None, ("gx", "gy")),
        P(None, ("gx", "gy")),
        P(None, ("gx", "gy")),
        P(("gx", "gy")),
        P(None, ("gx", "gy")),
    )
    return jax.shard_map(
        per_device,
        mesh=mesh,
        in_specs=placed,
        out_specs=(P(None, "gx", "gy", None), P(None, ("gx", "gy"))),
        check_vma=False,
    )
```

```python
import jax
import jax.numpy as jnp
from jax import lax
from jax.experimental import pallas as pl
from jax.experimental.pallas import tpu as pltpu
from jax.sharding import PartitionSpec as P

lattice_speeds = [
    (0, 0, 0),
    (1, 0, 0),
    (-1, 0, 0),
    (0, 1, 0),
    (0, -1, 0),
    (0, 0, 1),
    (0, 0, -1),
    (1, 1, 0),
    (-1, -1, 0),
    (1, -1, 0),
    (-1, 1, 0),
    (1, 0, 1),
    (-1, 0, -1),
    (1, 0, -1),
    (-1, 0, 1),
    (0, 1, 1),
    (0, -1, -1),
    (0, 1, -1),
    (0, -1, 1),
]
lattice_weights = [1.0 / 3.0] + [1.0 / 18.0] * 6 + [1.0 / 36.0] * 12
relax_time = 0.9
run = 128
sides = [(1, 1), (1, -1), (-1, 1), (-1, -1), (0, 1), (0, -1), (1, 0), (-1, 0)]
f32, bf16 = jnp.float32, jnp.bfloat16


def outer_weight(r):
    return (5.0 - 2.0 * r - jnp.sqrt(-7.0 + 12.0 * r - 4.0 * r * r)) / 8.0


def inner_weight(r):
    return (3.0 - 2.0 * r + jnp.sqrt(1.0 + 4.0 * r - 4.0 * r * r)) / 8.0


def up8(n):
    return (n + 7) // 8 * 8


class Plan:
    def __init__(self, wx, wy):
        self.wx, self.wy = wx, wy
        self.own = wx * wy
        self.xh = self.own
        self.yh = self.xh + 4 * wy
        self.co = self.yh + 3 * wx
        self.rows = self.co + 16
        hx, hy = [-1, wx, wx + 1], [-1, wy, wy + 1]
        self.row = {}
        for x in range(wx):
            for y in range(wy):
                self.row[x, y] = x * wy + y
        for k in range(3):
            for y in range(wy):
                self.row[hx[k], y] = self.xh + k * wy + y
            for x in range(wx):
                self.row[x, hy[k]] = self.yh + k * wx + x
            for m in range(3):
                self.row[hx[m], hy[k]] = self.co + 3 * k + m
        self.pads = [(self.xh + 3 * wy, wy), (self.co + 9, 7)]

        def span(d, w):
            full = list(range(w)) + [-1, w, w + 1]
            return {0: full, 1: [w - 1, w, w + 1], -1: [-1, 0, 1]}[d]

        def edge(d, w):
            return {0: list(range(w)), 1: [w - 1], -1: [0, 1]}[d]

        def near(d, w):
            return {0: list(range(w)), 1: [w - 1], -1: [0]}[d]

        def cells(d, pick):
            xs, ys = pick(d[0], wx), pick(d[1], wy)
            if d[1]:
                return [(x, y) for y in ys for x in xs]
            return [(x, y) for x in xs for y in ys]

        self.force = [cells(d, span) for d in sides]
        self.edge = [cells(d, edge) for d in sides]
        self.near = [cells(d, near) for d in sides]
        self.dirs = [
            [
                q
                for q, c in enumerate(lattice_speeds)
                if (not d[0] or c[0] == d[0]) and (not d[1] or c[1] == d[1])
            ]
            for d in sides
        ]
        self.force_rows = [up8(3 * len(c)) for c in self.force]
        self.macro_rows = [
            up8(4 * len(e) + len(q) * len(n)) for e, q, n in zip(self.edge, self.dirs, self.near)
        ]

    def there(self, cell, d):
        return self.row[cell[0] - d[0] * self.wx, cell[1] - d[1] * self.wy]


def runs(src, dst):
    out, i = [], 0
    while i < len(src):
        n, a, b = 1, 1, 1
        if i + 1 < len(src) and src[i + 1] > src[i] and dst[i + 1] > dst[i]:
            a, b = src[i + 1] - src[i], dst[i + 1] - dst[i]
            n = 2
            while i + n < len(src) and src[i + n] - src[i + n - 1] == a and dst[i + n] - dst[i + n - 1] == b:
                n += 1
        out.append((src[i], a, dst[i], b, n))
        i += n
    return out


def ds(start, n, stride):
    return pl.ds(start, n, stride=stride) if stride > 1 else pl.ds(start, n)


def move(src_ref, src, dst_ref, dst, add=False):
    for s, a, d, b, n in runs(src, dst):
        value = src_ref[ds(s, n, a), :]
        if add:
            value = value + dst_ref[ds(d, n, b), :]
        dst_ref[ds(d, n, b), :] = value


def split(value):
    high = value.astype(bf16)
    return high, (value - high.astype(f32)).astype(bf16)


def pick4(delta, weights):
    out = jnp.zeros(delta.shape, f32)
    for k in range(4):
        out = jnp.where(delta == k, weights[k], out)
    return out


def exchange_kernel(plan, nx, ny, *refs):
    wx, wy, rows, own = plan.wx, plan.wy, plan.rows, plan.own
    sources, results, scratch = refs[0:6], refs[6:12], refs[12:]
    pops, ext, grid, halo, plane, along = results
    ms, mr, fs, fr = scratch[0:8], scratch[8:16], scratch[16:24], scratch[24:32]
    base, frac, edges, stiff, rest, pos, pull, mem, sems, load_sems = scratch[32:]
    targets = (pops, base, frac, edges, stiff, rest)
    loads_in = [pltpu.make_async_copy(sources[n], targets[n], load_sems.at[n]) for n in range(6)]
    for n in (3, 2, 1, 5, 4, 0):
        loads_in[n].start()
    count, depth = base.shape[1], pops.shape[1]
    edge_count = edges.shape[1]
    tiles = count // run
    ix, iy = lax.axis_index("gx"), lax.axis_index("gy")
    peers = [(lax.rem(ix + dx + nx, nx), lax.rem(iy + dy + ny, ny)) for dx, dy in sides]
    barrier = pltpu.get_barrier_semaphore()
    for peer in peers:
        pl.semaphore_signal(barrier, inc=1, device_id=peer, device_id_type=pl.DeviceIdType.MESH)

    def copies(src, dst, kind):
        return [
            pltpu.make_async_remote_copy(
                src_ref=src[n],
                dst_ref=dst[n],
                send_sem=sems.at[kind, n],
                recv_sem=sems.at[kind + 1, n],
                device_id=peers[n],
                device_id_type=pl.DeviceIdType.MESH,
            )
            for n in range(8)
        ]

    macro_copies = copies(ms, mr, 0)
    force_copies = copies(fs, fr, 2)

    pos[...] = jnp.zeros(pos.shape, f32)
    pull[...] = jnp.zeros(pull.shape, f32)
    for n in (3, 2, 1, 5, 4):
        loads_in[n].wait()
    part = 8 * tiles
    moved = frac[...]
    high = moved.astype(bf16).astype(f32)
    low = moved - high
    whole = base[...].astype(f32)
    for t in range(tiles):
        cols = slice(t * run, (t + 1) * run)
        pos[pl.ds(8 * t, 3), :] = whole[:, cols]
        pos[pl.ds(part + 8 * t, 3), :] = high[:, cols]
        pos[pl.ds(2 * part + 8 * t, 3), :] = low[:, cols]
    ends = edges[...]
    spot = lax.broadcasted_iota(jnp.int32, (run, edge_count), 0)
    tail = jnp.bitwise_and(ends[0:1], run - 1)
    head = jnp.bitwise_and(ends[1:2], run - 1)
    hot = (jnp.where(spot == head, 1.0, 0.0) - jnp.where(spot == tail, 1.0, 0.0)).astype(bf16)
    group = lax.shift_right_logical(ends[0:1], run.bit_length() - 1)
    reach = jnp.dot(pos[...].astype(bf16), hot, preferred_element_type=f32)
    reach = reach[0:part] + reach[part : 2 * part] + reach[2 * part : 3 * part]
    pull[pl.ds(0, 3), :] = rest[...]
    diff = jnp.zeros((8, edge_count), f32)
    for t in range(tiles):
        diff = jnp.where(group == t, reach[8 * t : 8 * t + 8], diff)
    stretch = stiff[...].reshape(1, edge_count) * (diff - pull[...])
    terms = jnp.concatenate([jnp.where(group == t, stretch, 0.0) for t in range(tiles)], axis=0)
    big, small = split(terms)
    both = jnp.concatenate([big, small], axis=0)
    summed = lax.dot_general(both, hot, (((1,), (1,)), ((), ())), preferred_element_type=f32)
    summed = summed[0:part] + summed[part : 2 * part]
    for t in range(tiles):
        mem[:, t * run : (t + 1) * run] = -summed[8 * t : 8 * t + 8]

    weights = [
        outer_weight(1.0 + moved),
        inner_weight(moved),
        inner_weight(1.0 - moved),
        outer_weight(2.0 - moved),
    ]
    bx = base[0:1, :] - ix * wx - 1
    by = base[1:2, :] - iy * wy - 1
    bz = base[2:3, :] - 1
    gap = lax.broadcasted_iota(jnp.int32, (depth, count), 0) - bz
    gap = jnp.where(gap < 0, gap + depth, gap)
    gap = jnp.where(gap >= depth, gap - depth, gap)
    along_z = pick4(gap, [w[2:3] for w in weights])
    z_high, z_low = split(along_z)
    along[pl.ds(0, depth), :] = z_high
    along[pl.ds(depth, depth), :] = z_low
    far = -100
    for r in range(0, rows, 16):
        i = lax.broadcasted_iota(jnp.int32, (16, 1), 0)
        if r < plan.xh:
            i = i + r
            x = i // wy
            y = i - x * wy
        elif r < plan.yh:
            i = i + (r - plan.xh)
            k = i // wy
            x = jnp.where(k == 0, -1, jnp.where(k == 3, far, wx - 1 + k))
            y = i - k * wy
        elif r < plan.co:
            k = (r - plan.yh) // wx
            x = i + (r - plan.yh - k * wx)
            y = jnp.full((16, 1), (-1, wy, wy + 1)[k], jnp.int32)
        else:
            k = jnp.where(i >= 6, 2, jnp.where(i >= 3, 1, 0))
            m = i - 3 * k
            x = jnp.where(m == 0, -1, jnp.where(m >= 3, far, wx - 1 + m))
            y = jnp.where(k == 0, -1, wy - 1 + k)
        px = pick4(x - bx, [w[0:1] for w in weights])
        py = pick4(y - by, [w[1:2] for w in weights])
        plane[pl.ds(r, 16), :] = px * py
    flat = plane[...]
    loads = [split(flat * mem[c : c + 1, :]) for c in range(3)]
    stack = jnp.concatenate([h for h, _ in loads] + [l for _, l in loads], axis=0)
    spread = lax.dot_general(stack, along[...], (((1,), (1,)), ((), ())), preferred_element_type=f32)
    spread = spread[0 : 3 * rows] + spread[3 * rows : 6 * rows]
    grid[...] = spread[:, 0:depth] + spread[:, depth : 2 * depth]
    for n in range(8):
        cells = plan.force[n]
        for k in range(3):
            move(grid, [k * rows + plan.row[c] for c in cells], fs[n], [k * len(cells) + i for i in range(len(cells))])
    loads_in[0].wait()
    for r in range(0, own, 16):
        totals = [None] * 4
        for q, c in enumerate(lattice_speeds):
            value = pops[pl.ds(q * own + r, 16), :]
            for k, sign in enumerate((1,) + c):
                if sign:
                    term = value if sign > 0 else -value
                    totals[k] = term if totals[k] is None else totals[k] + term
        for k in range(4):
            ext[pl.ds(k * rows + r, 16), :] = totals[k]
    for start, n in plan.pads:
        for k in range(4):
            ext[pl.ds(k * rows + start, n), :] = jnp.full((n, depth), 0.0 if k else 1.0, f32)
    for n in range(8):
        cells, close = plan.edge[n], plan.near[n]
        for k in range(4):
            move(ext, [k * rows + plan.row[c] for c in cells], ms[n], [k * len(cells) + i for i in range(len(cells))])
        for s, q in enumerate(plan.dirs[n]):
            first = 4 * len(cells) + s * len(close)
            move(pops, [q * own + plan.row[c] for c in close], ms[n], [first + i for i in range(len(close))])

    pl.semaphore_wait(barrier, 8)
    for copy in macro_copies:
        copy.start()

    for copy in force_copies:
        copy.start()

    for n in range(8):
        macro_copies[n].wait_recv()
        cells, close, d = plan.edge[n], plan.near[n], sides[n]
        for k in range(4):
            move(mr[n], [k * len(cells) + i for i in range(len(cells))], ext, [k * rows + plan.there(c, d) for c in cells])
        for s, q in enumerate(plan.dirs[n]):
            first = 4 * len(cells) + s * len(close)
            move(mr[n], [first + i for i in range(len(close))], halo, [q * rows + plan.there(c, d) for c in close])
    for n in range(8):
        force_copies[n].wait_recv()
        cells, d = plan.force[n], sides[n]
        for k in range(3):
            move(fr[n], [k * len(cells) + i for i in range(len(cells))], grid, [k * rows + plan.there(c, d) for c in cells], add=True)

    for copy in macro_copies + force_copies:
        copy.wait_send()


def collide_kernel(plan, pops, ext, grid, halo, plane, along, fresh_out, sampled_out, *scratch):
    wx, wy, rows, own = plan.wx, plan.wy, plan.rows, plan.own
    fresh, sampled, post, vel, sems = scratch
    depth = pops.shape[1]
    leave = [
        pltpu.make_async_copy(
            fresh.at[pl.ds(q * own, own), :], fresh_out.at[pl.ds(q * own, own), :], sems.at[q]
        )
        for q in range(19)
    ]
    leave.append(pltpu.make_async_copy(sampled, sampled_out, sems.at[19]))
    keep = 1.0 - 1.0 / relax_time
    half = 1.0 - 0.5 / relax_time

    def along_speed(c, vector):
        total = None
        for k in range(3):
            if c[k]:
                term = vector[k] if c[k] > 0 else -vector[k]
                total = term if total is None else total + term
        return total

    for r in range(0, rows, 16):
        density = ext[pl.ds(r, 16), :]
        force = [grid[pl.ds(k * rows + r, 16), :] for k in range(3)]
        inverse = 1.0 / density
        speed = [(ext[pl.ds((k + 1) * rows + r, 16), :] + 0.5 * force[k]) * inverse for k in range(3)]
        for k in range(3):
            vel[pl.ds(k * rows + r, 16), :] = speed[k]
        if r < own:
            need = list(range(19))
        elif r < plan.yh:
            need = [q for q in range(19) if lattice_speeds[q][0]]
        elif r < plan.yh + wx:
            need = [q for q in range(19) if lattice_speeds[q][1] == 1]
        elif r < plan.yh + 2 * wx:
            need = [q for q in range(19) if lattice_speeds[q][1] == -1]
        elif r < plan.co:
            continue
        else:
            need = [q for q in range(19) if lattice_speeds[q][0] and lattice_speeds[q][1]]
        square = speed[0] * speed[0] + speed[1] * speed[1] + speed[2] * speed[2]
        work = speed[0] * force[0] + speed[1] * force[1] + speed[2] * force[2]
        scaled = density * (1.0 / relax_time)
        level = scaled * (1.0 - 1.5 * square) - (3.0 * half) * work
        for first in [0] + list(range(1, 19, 2)):
            pair = [0] if first == 0 else [first, first + 1]
            if not any(q in need for q in pair):
                continue
            weight = lattice_weights[first]
            if first == 0:
                even, odd = level * weight, None
            else:
                a = along_speed(lattice_speeds[first], speed)
                push = along_speed(lattice_speeds[first], force)
                turn = scaled * a + half * push
                even = weight * (level + a * (4.5 * scaled * a + 9.0 * half * push))
                odd = (3.0 * weight) * turn
            for q in pair:
                if q not in need:
                    continue
                c = lattice_speeds[q]
                if r < own:
                    value = pops[pl.ds(q * own + r, 16), :]
                else:
                    value = halo[pl.ds(q * rows + r, 16), :]
                value = keep * value + even
                if odd is not None:
                    value = value + odd if q == first else value - odd
                if c[2]:
                    value = pltpu.roll(value, c[2] % depth, 1)
                if c[0] == 0 and c[1] == 0:
                    fresh[pl.ds(q * own + r, 16), :] = value
                else:
                    post[pl.ds(q * rows + r, 16), :] = value
    for q, c in enumerate(lattice_speeds):
        if c[0] == 0 and c[1] == 0:
            leave[q].start()
            continue
        if c[1]:
            cells = [(x, y) for y in range(wy) for x in range(wx)]
        else:
            cells = [(x, y) for x in range(wx) for y in range(wy)]
        move(
            post,
            [q * rows + plan.row[x - c[0], y - c[1]] for x, y in cells],
            fresh,
            [q * own + x * wy + y for x, y in cells],
        )
        leave[q].start()

    v_high, v_low = split(vel[...])
    value = jnp.dot(v_high, along[pl.ds(0, depth), :], preferred_element_type=f32)
    value = value + jnp.dot(v_low, along[pl.ds(0, depth), :], preferred_element_type=f32)
    value = value + jnp.dot(v_high, along[pl.ds(depth, depth), :], preferred_element_type=f32)
    flat = plane[...]
    for k in range(3):
        sampled[k : k + 1, :] = jnp.sum(value[k * rows : (k + 1) * rows] * flat, axis=0, keepdims=True)
    leave[19].start()
    for copy in leave:
        copy.wait()


def solution(mesh):
    nx, ny = mesh.shape["gx"], mesh.shape["gy"]

    def per_device(populations, vert_base, vert_frac, edges, stiffness, rest):
        _, wx, wy, depth = populations.shape
        count, edge_count = vert_base.shape[1], edges.shape[1]
        plan = Plan(wx, wy)
        rows, tiles = plan.rows, count // run
        macro = [pltpu.VMEM((n, depth), f32) for n in plan.macro_rows]
        force = [pltpu.VMEM((n, depth), f32) for n in plan.force_rows]
        scratch = macro + macro + force + force
        scratch += [
            pltpu.VMEM((3, count), jnp.int32),
            pltpu.VMEM((3, count), f32),
            pltpu.VMEM((2, edge_count), jnp.int32),
            pltpu.VMEM((edge_count,), f32),
            pltpu.VMEM((3, edge_count), f32),
            pltpu.VMEM((24 * tiles, run), f32),
            pltpu.VMEM((8, edge_count), f32),
            pltpu.VMEM((8, count), f32),
            pltpu.SemaphoreType.DMA((4, 8)),
            pltpu.SemaphoreType.DMA((6,)),
        ]
        vmem = pl.BlockSpec(memory_space=pltpu.VMEM)
        far = pl.BlockSpec(memory_space=pltpu.HBM)

        def exchange(*refs):
            exchange_kernel(plan, nx, ny, *refs)

        def collide(*refs):
            collide_kernel(plan, *refs)

        held = pl.pallas_call(
            exchange,
            out_shape=(
                jax.ShapeDtypeStruct((19 * wx * wy, depth), f32),
                jax.ShapeDtypeStruct((4 * rows, depth), f32),
                jax.ShapeDtypeStruct((3 * rows, depth), f32),
                jax.ShapeDtypeStruct((19 * rows, depth), f32),
                jax.ShapeDtypeStruct((rows, count), f32),
                jax.ShapeDtypeStruct((2 * depth, count), bf16),
            ),
            in_specs=[far] * 6,
            out_specs=(vmem,) * 6,
            scratch_shapes=scratch,
            compiler_params=pltpu.CompilerParams(
                collective_id=0, has_side_effects=True, vmem_limit_bytes=24 * 1024 * 1024
            ),
            name="exchange",
        )(
            *[
                pltpu.with_memory_space_constraint(value, pltpu.HBM)
                for value in (
                    populations.reshape(19 * wx * wy, depth),
                    vert_base,
                    vert_frac,
                    edges,
                    stiffness,
                    rest,
                )
            ]
        )
        fresh, sampled = pl.pallas_call(
            collide,
            out_shape=(
                jax.ShapeDtypeStruct((19 * wx * wy, depth), f32),
                jax.ShapeDtypeStruct((3, count), f32),
            ),
            in_specs=[vmem] * 6,
            out_specs=(far, far),
            scratch_shapes=[
                pltpu.VMEM((19 * wx * wy, depth), f32),
                pltpu.VMEM((3, count), f32),
                pltpu.VMEM((19 * rows, depth), f32),
                pltpu.VMEM((3 * rows, depth), f32),
                pltpu.SemaphoreType.DMA((20,)),
            ],
            compiler_params=pltpu.CompilerParams(vmem_limit_bytes=24 * 1024 * 1024),
            name="collide",
        )(*held)
        return fresh.reshape(19, wx, wy, depth), sampled

    placed = (
        P(None, "gx", "gy", None),
        P(None, ("gx", "gy")),
        P(None, ("gx", "gy")),
        P(None, ("gx", "gy")),
        P(("gx", "gy")),
        P(None, ("gx", "gy")),
    )
    return jax.shard_map(
        per_device,
        mesh=mesh,
        in_specs=placed,
        out_specs=(P(None, "gx", "gy", None), P(None, ("gx", "gy"))),
        check_vma=False,
    )
```
